32 devices in a mesh: parts: 2 (over y), samp: 4 (over x, core), bond: 4 (over z).
Axes of the slice: x: 2, y: 2, z: 4, core: 2. Of those that a mesh axis runs over, the one named last changes fastest.
Arguments:
- env_start: bfloat16 [4096, 4096], P(('parts', 'samp'), 'bond'), parts along dimension 0, may hold values from -6 to 6
- stored_sites: bfloat16 [4, 4, 1024, 4, 4096], P('parts', 'samp', None, None, 'bond'), parts along dimension 0, may hold values from -1 to 1
- slab_order: int32 [4, 4], P('parts'), parts along dimension 0, may hold values from 0 to 3, each once within a row
- chosen: int32 [4096, 2], P(('parts', 'samp')), parts along dimension 0, may hold values from 0 to 3
Outputs:
- probabilities: float32 [4096, 2, 4], P(('parts', 'samp')), parts along dimension 0
- env_final: float32 [4096, 4096], P(('parts', 'samp'), 'bond'), parts along dimension 0
The draws below stay inside these ranges and needn't reach their ends.
There are 2 independent parts, one for each index of `parts`. The reference program is written for one: setup_inputs(seed, part) draws one part's arguments, and reference() takes and returns one part's arrays. A program takes and returns all parts, laid end to end along the dimension named above; each array names one. Nothing has to cross between parts.
Inputs may be any that keep to these rules, and one draw needn't show every extreme that they name: Each row of slab_order names every index of samp once.
All inputs are finite; a program needn't handle non-finite values.
Results may differ from the reference program's by a relative error of at most 0.005.
Values may be sent and summed in bfloat16 or wider, within the bound.
A program may use at most 192 MiB of HBM per device.

```python
import math
import jax
import jax.numpy as jnp
from jax import lax

CHI = 4096
D_F = 4
STEPS = 2
SAMPLES = 2048
SLAB = 1024
N_SAMP = 4


def draw_stored_sites(key, part):
    key_base = jax.random.fold_in(key, 11)
    key_cols = jax.random.fold_in(key, 12)
    base = jnp.clip(jax.random.normal(key_base, (STEPS, N_SAMP, SLAB, D_F, CHI), jnp.float32), -6.0, 6.0)
    position = jnp.arange(CHI, dtype=jnp.float32) / max(CHI - 1, 1)
    col_scale = jnp.exp(jax.random.uniform(key_cols, (CHI,), jnp.float32, 0.0, math.log(10.0)))
    col_scale = col_scale * jnp.exp(0.5 * math.log(3.0) * position)
    scaled = base * col_scale / (4.0 * math.sqrt(CHI))
    return jnp.clip(scaled, -1.0, 1.0).astype(jnp.bfloat16)


def with_ends(values, own_key, least, top_value):
    dims = values.shape
    spot = [jax.random.randint(jax.random.fold_in(own_key, axis), (), 0, dims[axis]) for axis in range(len(dims))]
    values = values.at[tuple(spot)].set(least)
    longest = dims.index(max(dims))
    spot[longest] = (spot[longest] + 1) % dims[longest]
    return values.at[tuple(spot)].set(top_value)


def shard_levels(own_key, shape, cuts, smallest, top_value):
    gain, own = 1.0, jax.random.fold_in(own_key, 6)
    for axis_at, parts in cuts:
        draws = jnp.exp(jax.random.uniform(jax.random.fold_in(own, axis_at), (parts,), jnp.float32, smallest / len(cuts), top_value / len(cuts)))
        gain = gain * jnp.repeat(draws, shape[axis_at] // parts).reshape([-1 if axis == axis_at else 1 for axis in range(len(shape))])
    return gain


def gaussian(rng, extent, spread, most, pieces=(), kind=jnp.bfloat16):
    level = shard_levels(rng, extent, pieces, -0.22, 0.18) if pieces else 1.0
    drawn = jax.random.normal(rng, extent, jnp.float32) * spread * level
    return jnp.minimum(jnp.maximum(drawn, -most), most).astype(kind)


def setup_inputs(seed: int = 0, part: int = 0) -> dict:
    key_of = jax.random.split(jax.random.key(seed), 5)
    part_keys = jax.random.split(jax.random.fold_in(key_of[4], part), 5)
    return {
        "env_start": gaussian(part_keys[0], (SAMPLES, CHI), 1.0, 6.0, ((0, 4), (1, 4))),
        "stored_sites": draw_stored_sites(jax.random.fold_in(jax.random.fold_in(key_of[4], part), 71), part),
        "slab_order": jax.vmap(lambda own: jax.random.permutation(own, N_SAMP))(jax.random.split(part_keys[2], STEPS)).reshape((STEPS, N_SAMP)).astype(jnp.int32),
        "chosen": with_ends(jax.random.randint(part_keys[3], (SAMPLES, STEPS), 0, D_F), jax.random.fold_in(part_keys[3], 1), 0, D_F - 1).astype(jnp.int32),
    }


epsilon = 1e-06

def reference(env_start, stored_sites, slab_order, chosen):
    samples = env_start.shape[0]
    raw_env = env_start
    factor = jnp.ones((samples,), jnp.float32)
    outcomes = jnp.arange(D_F, dtype=jnp.int32)
    prob_list = []
    selected = None
    for site_index in range(STEPS):
        blocks = raw_env.reshape(samples, N_SAMP, SLAB)
        ordered = jnp.take(blocks, slab_order[site_index].astype(jnp.int32), axis=1).reshape(samples, CHI)
        site_block = stored_sites[site_index].reshape(CHI, D_F * CHI)
        product = jnp.dot(ordered, site_block, preferred_element_type=jnp.float32).reshape(samples, D_F, CHI)
        amplitude = product * factor[:, None, None]
        totals = lax.optimization_barrier(jnp.sum(amplitude * amplitude, axis=2))
        prob_list.append(totals / lax.optimization_barrier(jnp.sum(totals, axis=1, keepdims=True)))
        selector = (chosen[:, site_index][:, None] == outcomes[None, :]).astype(jnp.float32)
        selected = jnp.einsum('sn,snc->sc', selector, product)
        chosen_total = lax.optimization_barrier(jnp.sum(totals * selector, axis=1))
        factor = factor * lax.rsqrt(chosen_total / CHI + epsilon)
        if site_index + 1 < STEPS:
            raw_env = selected.astype(jnp.bfloat16)
    env_final = selected * factor[:, None]
    return (jnp.stack(prob_list, axis=1), env_final)
```

```python
import functools

import jax
import jax.numpy as jnp
from jax import lax
from jax.experimental import pallas as pl
from jax.experimental.pallas import tpu as pltpu
from jax.sharding import PartitionSpec as P


STEPS = 2
CHUNKS = 2
PIECES = 2
epsilon = 1e-06


def tile_of(width):
    return min(width, 256)


def dots(env_ref, weight_refs, outcome):
    total = None
    for part, weight_ref in enumerate(weight_refs):
        term = jnp.dot(env_ref[part], weight_ref[outcome], preferred_element_type=jnp.float32)
        total = term if total is None else total + term
    return total


def product_kernel(count, env_ref, *refs):
    weight_refs, out_ref = refs[:count], refs[count]
    for outcome in range(out_ref.shape[0]):
        out_ref[outcome] = dots(env_ref, weight_refs, outcome).astype(out_ref.dtype)


def product(env, weights, piece, pieces, dtype):
    outcomes, rows, width = weights[0].shape
    count = outcomes // pieces
    samples, tile = env.shape[1], tile_of(width)
    flops = 2 * samples * sum(w.size for w in weights) // pieces
    moved = 2 * sum(w.size for w in weights) // pieces
    return pl.pallas_call(
        functools.partial(product_kernel, len(weights)),
        grid=(width // tile,),
        in_specs=[pl.BlockSpec(env.shape, lambda t: (0, 0, 0))]
        + [pl.BlockSpec((count, rows, tile), lambda t: (piece, 0, t)) for _ in weights],
        out_specs=pl.BlockSpec((count, samples, tile), lambda t: (0, 0, t)),
        out_shape=jax.ShapeDtypeStruct((count, samples, width), dtype),
        cost_estimate=pl.CostEstimate(flops=flops, bytes_accessed=moved, transcendentals=0),
    )(env, *weights)


def finish_kernel(pieces, site, own_ref, chosen_ref, before_ref, *refs):
    other_refs, (totals_ref, selected_ref) = refs[:-2], refs[-2:]
    outcomes = own_ref.shape[0]
    each = outcomes // pieces

    @pl.when(pl.program_id(0) == 0)
    def _():
        totals_ref[...] = before_ref[...]

    lane = lax.broadcasted_iota(jnp.int32, totals_ref.shape, 1)
    selected = None
    added = jnp.zeros(totals_ref.shape, jnp.float32)
    for outcome in range(outcomes):
        total = own_ref[outcome]
        for other_ref in other_refs[outcome // each :: pieces]:
            total = total + other_ref[outcome % each].astype(jnp.float32)
        norm = jnp.sum(total * total, axis=1, keepdims=True)
        added = jnp.where(lane == site * outcomes + outcome, norm, added)
        hit = chosen_ref[...] == outcome
        selected = jnp.where(hit, total, 0.0 if selected is None else selected)
    totals_ref[...] += added
    selected_ref[...] = selected.astype(selected_ref.dtype)


def finish(own, others, chosen, before, site, dtype):
    outcomes, samples, width = own.shape
    tile = tile_of(width)
    pieces = outcomes // others[0].shape[0] if others else 1
    return pl.pallas_call(
        functools.partial(finish_kernel, pieces, site),
        grid=(width // tile,),
        in_specs=[
            pl.BlockSpec((outcomes, samples, tile), lambda t: (0, 0, t)),
            pl.BlockSpec((samples, 1), lambda t: (0, 0)),
            pl.BlockSpec((samples, 128), lambda t: (0, 0)),
        ]
        + [pl.BlockSpec((outcomes // pieces, samples, tile), lambda t: (0, 0, t)) for _ in others],
        out_specs=(
            pl.BlockSpec((samples, 128), lambda t: (0, 0)),
            pl.BlockSpec((samples, tile), lambda t: (0, t)),
        ),
        out_shape=(
            jax.ShapeDtypeStruct((samples, 128), jnp.float32),
            jax.ShapeDtypeStruct((samples, width), dtype),
        ),
        cost_estimate=pl.CostEstimate(
            flops=4 * own.size, bytes_accessed=8 * own.size, transcendentals=0
        ),
    )(own, chosen, before, *others)


def relayout_kernel(stored_ref, _, out_ref):
    for outcome in range(out_ref.shape[0]):
        out_ref[outcome] = stored_ref[0, 0, :, outcome, :]


def relayout(stored_sites, site, after):
    rows, outcomes, width = stored_sites.shape[2:]
    tile = min(rows, 128)
    return pl.pallas_call(
        relayout_kernel,
        grid=(rows // tile,),
        in_specs=[
            pl.BlockSpec((1, 1, tile, outcomes, width), lambda t: (site, 0, t, 0, 0)),
            pl.BlockSpec(memory_space=pl.ANY),
        ],
        out_specs=pl.BlockSpec((outcomes, tile, width), lambda t: (0, t, 0)),
        out_shape=jax.ShapeDtypeStruct((outcomes, rows, width), stored_sites.dtype),
        cost_estimate=pl.CostEstimate(
            flops=0, bytes_accessed=4 * rows * outcomes * width, transcendentals=0
        ),
    )(stored_sites, after)


def pick_kernel(inner, index_ref, *refs):
    pieces, outs = refs[: len(refs) - inner[1]], refs[len(refs) - inner[1] :]
    for target, out_ref in enumerate(outs):
        for part in range(inner[0]):
            for source, piece_ref in enumerate(pieces):

                @pl.when(index_ref[target * inner[0] + part] == source)
                def _():
                    out_ref[part] = piece_ref[...]


def pick_blocks(index, pieces, outer, inner):
    samples, width = pieces[0].shape
    spec = pl.BlockSpec((samples, width), lambda t, index: (0, 0))
    return pl.pallas_call(
        functools.partial(pick_kernel, (inner, outer)),
        grid_spec=pltpu.PrefetchScalarGridSpec(
            num_scalar_prefetch=1,
            grid=(1,),
            in_specs=[spec] * len(pieces),
            out_specs=[pl.BlockSpec((inner, samples, width), lambda t, index: (0, 0, 0))] * outer,
        ),
        out_shape=[jax.ShapeDtypeStruct((inner, samples, width), pieces[0].dtype)] * outer,
        cost_estimate=pl.CostEstimate(
            flops=0, bytes_accessed=2 * samples * width * (len(pieces) + outer * inner), transcendentals=0
        ),
    )(index, *pieces)


def compute(env_start, stored_sites, slab_order, chosen):
    groups = slab_order.shape[1]
    inner = 2 if groups % 2 == 0 else 1
    outer = groups // inner
    bonds = lax.axis_size("bond")
    mine, place = lax.axis_index("samp"), lax.axis_index("bond")
    core, chip = mine % inner, mine // inner
    rows, outcomes, width = stored_sites.shape[2:]
    bond_width = width * bonds
    samples = env_start.shape[0]
    chunks = CHUNKS if samples % (CHUNKS * 16) == 0 else 1
    size = samples // chunks

    def across(value, step):
        return lax.ppermute(
            value, "samp", [(i, ((i // inner + step) % outer) * inner + i % inner) for i in range(groups)]
        )

    def inside(value, step):
        return lax.ppermute(
            value, "samp", [((i // inner) * inner + (i + step) % inner, i) for i in range(groups)]
        )

    def along(value, step):
        return lax.ppermute(value, "bond", [(i, (i + step) % bonds) for i in range(bonds)])

    def load(site, after):
        own = relayout(stored_sites, site, after)
        return [own] + [inside(own, step) for step in range(1, inner)]

    wanted = [
        jnp.stack(
            [
                slab_order[site, ((chip + step) % outer) * inner + (core + part) % inner]
                for step in range(outer)
                for part in range(inner)
            ]
        )
        for site in range(STEPS)
    ]

    def gather(value, site):
        if bonds == groups:
            pieces = [value] + [along(value, step) for step in range(1, bonds)]
            index = (place - wanted[site] + bonds) % bonds
            return lambda: pick_blocks(index, pieces, outer, inner)
        whole = lax.all_gather(value, "bond", axis=1, tiled=True)
        blocks = [
            lax.dynamic_slice_in_dim(whole, wanted[site][i] * rows, rows, axis=1)
            for i in range(groups)
        ]
        return lambda: [
            jnp.stack(blocks[step * inner : (step + 1) * inner]) for step in range(outer)
        ]

    def bond_sum(value):
        if bonds <= 4:
            return sum([along(value, step) for step in range(1, bonds)], value)
        return lax.psum(value, "bond")

    raws = [env_start[c * size : (c + 1) * size] for c in range(chunks)]
    picks = [chosen[c * size : (c + 1) * size] for c in range(chunks)]
    norms = [jnp.zeros((size, 128), jnp.float32)] * chunks

    def fetch(value, site):
        pick = gather(value, site)
        own, *foreign = pick()
        return own, [(i + 1, across(block, i + 1)) for i, block in enumerate(foreign)]

    owns, sents = [], []
    for c in range(chunks):
        own, sent = fetch(raws[c], 0)
        owns.append(own)
        sents.append(sent)
    weights = load(0, norms[0])
    for site in range(STEPS):
        last = site + 1 == STEPS
        answers = []
        for c in range(chunks):
            parts, anchor = [], norms[0]
            for step, foreign in sents[c]:
                for piece in range(PIECES):
                    anchor = product(foreign, weights, piece, PIECES, jnp.bfloat16)
                    parts.append(across(anchor, -step))
            answers.append(parts)
            if c == 0 and not last:
                later = load(site + 1, anchor)
        new_owns, new_sents = [], []
        for c in range(chunks):
            own = product(owns[c], weights, 0, 1, jnp.float32)
            norms[c], raws[c] = finish(
                own,
                answers[c],
                picks[c][:, site : site + 1],
                norms[c],
                site,
                jnp.float32 if last else jnp.bfloat16,
            )
            if not last:
                own, sent = fetch(raws[c], site + 1)
                new_owns.append(own)
                new_sents.append(sent)
        if not last:
            owns, sents, weights = new_owns, new_sents, later
    sums = [bond_sum(norm) for norm in norms]
    totals = [[s[:, site * outcomes : (site + 1) * outcomes] for s in sums] for site in range(STEPS)]
    probabilities, finals = [], []
    labels = jnp.arange(outcomes, dtype=jnp.int32)
    for c in range(chunks):
        factor = jnp.ones((size,), jnp.float32)
        rows_out = []
        for site in range(STEPS):
            scaled = totals[site][c] * (factor * factor)[:, None]
            rows_out.append(scaled / jnp.sum(scaled, axis=1, keepdims=True))
            hit = picks[c][:, site][:, None] == labels[None, :]
            factor = factor * lax.rsqrt(jnp.sum(jnp.where(hit, scaled, 0.0), axis=1) / bond_width + epsilon)
        probabilities.append(jnp.stack(rows_out, axis=1))
        finals.append(raws[c] * factor[:, None])
    return jnp.concatenate(probabilities), jnp.concatenate(finals)


MESH = pl.DeviceIdType.MESH
PARTS_OF_SITE = 4
SHARE = 4
LEAD = 3


def sampling_kernel(
    bonds, groups, mask_ref, env_ref, stored_ref, chosen_ref, selected_ref, totals_ref,
    weights, blocks, foreign, picked, partial, answer, own, left, stage, norms, gathered,
    env_sem, stage_sem, weight_send, weight_recv, gather_send, gather_recv, cross_send, cross_recv,
    spread_send, spread_recv, answer_send, answer_recv, norm_send, norm_recv,
):
    mine, place = lax.axis_index("samp"), lax.axis_index("bond")
    core = lax.rem(mine, 2)
    sibling, opposite = mine + 1 - 2 * core, lax.rem(mine + groups // 2, groups)
    peers = (None, place + 1 - 2 * lax.rem(place, 2), lax.rem(place + 2, bonds), bonds - 1 - place)
    middle = lax.div(place + 1, 2) == 1
    outer = lax.div(place + 1, 2) != 1
    outcomes = weights.shape[2]
    width = weights.shape[4]
    chunks = PARTS_OF_SITE
    rows = left.shape[1] // 2
    share = rows // SHARE
    units = STEPS * chunks
    slab = weights.shape[3]
    tall = stage.shape[1]
    tiles = slab // tall
    strip = min(width, 256)
    band = min(rows, 16)

    def copy_to(src, dst, send, recv, where):
        return pltpu.make_async_remote_copy(
            src_ref=src, dst_ref=dst, send_sem=send, recv_sem=recv, device_id=where, device_id_type=MESH
        )

    def split(unit):
        return lax.div(unit, chunks), lax.rem(unit, chunks)

    def spot(chunk):
        return pl.ds(pl.multiple_of(chunk * rows, rows), rows)

    def hop(unit, d):
        site, chunk = split(unit)
        ref = blocks.at[site, place, spot(chunk)]
        return copy_to(ref, ref, gather_send.at[unit, d - 1], gather_recv.at[unit, d - 1], {"bond": peers[d]})

    def relay(unit):
        site, chunk = split(unit)
        ref = blocks.at[site, peers[3], spot(chunk)]
        return copy_to(ref, ref, gather_send.at[unit, 1], gather_recv.at[unit, 1], {"bond": peers[1]})

    def cross_whole(unit):
        return copy_to(
            picked.at[lax.rem(unit, 2)],
            foreign.at[lax.rem(unit, chunks)],
            cross_send.at[unit],
            cross_recv.at[unit],
            {"samp": opposite},
        )

    def band_of(position):
        return pl.ds(pl.multiple_of(position * share, share), share)

    def cross_part(unit):
        return copy_to(
            picked.at[lax.rem(unit, 2), :, pl.ds(0, share)],
            foreign.at[lax.rem(unit, chunks), :, band_of(lax.rem(place, SHARE))],
            cross_send.at[unit],
            cross_recv.at[unit],
            {"samp": opposite},
        )

    def spread(unit, d):
        ref = foreign.at[lax.rem(unit, chunks), :, band_of(lax.rem(place, SHARE))]
        return copy_to(ref, ref, spread_send.at[unit, d - 1], spread_recv.at[unit, d - 1], {"bond": peers[d]})

    def reply(unit, outcome):
        return copy_to(
            partial.at[lax.rem(unit, 2), outcome],
            answer.at[lax.rem(unit, chunks), outcome],
            answer_send.at[unit, outcome],
            answer_recv.at[unit, outcome],
            {"samp": opposite},
        )

    def load(index):
        return pltpu.make_async_copy(
            stored_ref.at[lax.div(index, tiles), 0, pl.ds(lax.rem(index, tiles) * tall, tall)],
            stage.at[lax.rem(index, 2)],
            stage_sem.at[lax.rem(index, 2)],
        )

    def trade(index):
        site, at = lax.div(index, tiles), pl.ds(pl.multiple_of(lax.rem(index, tiles) * tall, tall), tall)
        return copy_to(
            weights.at[site, 0, :, at],
            weights.at[site, 1, :, at],
            weight_send.at[site],
            weight_recv.at[site],
            {"samp": sibling},
        )

    def trade_all(site):
        return copy_to(
            weights.at[site, 0], weights.at[site, 1], weight_send.at[site], weight_recv.at[site], {"samp": sibling}
        )

    def pick(site, which, at):
        total = None
        for block in range(bonds):
            term = blocks[site, block, at, :].astype(jnp.float32) * mask_ref[(site * 4 + which) * bonds + block]
            total = term if total is None else total + term
        return total.astype(left.dtype)

    def send_blocks(unit):
        hop(unit, 1).start()
        hop(unit, 3).start()

        @pl.when(outer)
        def _():
            hop(unit, 2).start()

    def forward_block(unit):
        @pl.when(middle)
        def _():
            hop(unit, 3).wait_recv()
            relay(unit).start()

    def send_foreign(unit):
        site, chunk = split(unit)
        hop(unit, 1).wait_recv()
        hop(unit, 2).wait_recv()

        @pl.when(outer)
        def _():
            hop(unit, 3).wait_recv()

        slot = lax.rem(unit, 2)

        @pl.when(unit == 2)
        def _():
            cross_whole(unit - 2).wait_send()

        @pl.when(unit > 2)
        def _():
            cross_part(unit - 2).wait_send()

        @pl.when(unit == 0)
        def _():
            for part in range(2):

                @pl.loop(0, rows // band)
                def _(step):
                    at = pl.multiple_of(step * band, band)
                    picked[slot, part, pl.ds(at, band), :] = pick(site, 2 + part, pl.ds(chunk * rows + at, band))

            cross_whole(unit).start()

        @pl.when(unit > 0)
        def _():
            at = pl.multiple_of(chunk * rows + lax.rem(place, SHARE) * share, share)
            for part in range(2):
                picked[slot, part, pl.ds(0, share), :] = pick(site, 2 + part, pl.ds(at, share))
            cross_part(unit).start()

    def spread_foreign(unit):
        @pl.when(unit > 0)
        def _():
            cross_part(unit).wait_recv()
            for d in range(1, SHARE):
                spread(unit, d).start()

    def multiply(unit):
        site, chunk = split(unit)
        slot = lax.rem(unit, 2)

        for part in range(2):

            @pl.loop(0, rows // band)
            def _(step):
                at = pl.multiple_of(step * band, band)
                left[part, pl.ds(rows + at, band), :] = pick(site, part, pl.ds(chunk * rows + at, band))

        @pl.when(unit == 0)
        def _():
            cross_whole(unit).wait_recv()

        @pl.when(unit > 0)
        def _():
            for d in range(1, SHARE):
                spread(unit, d).wait_recv()
            for d in range(1, SHARE):
                spread(unit, d).wait_send()

        for part in range(2):
            left[part, pl.ds(0, rows), :] = foreign[chunk, part]

        @pl.when(chunk == 0)
        def _():
            trade_all(site).wait_recv()

        @pl.loop(0, outcomes)
        def _(outcome):
            @pl.when((outcome == outcomes // 2) & (unit + 1 < units))
            def _():
                spread_foreign(unit + 1)

            @pl.when(unit >= 2)
            def _():
                reply(unit - 2, outcome).wait_send()

            @pl.loop(0, width // strip)
            def _(step):
                at = pl.ds(pl.multiple_of(step * strip, strip), strip)
                total = jnp.dot(left[0], weights[site, 0, outcome, :, at], preferred_element_type=jnp.float32)
                total = total + jnp.dot(left[1], weights[site, 1, outcome, :, at], preferred_element_type=jnp.float32)
                partial[slot, outcome, :, at] = total[:rows].astype(partial.dtype)
                own[slot, outcome, :, at] = total[rows:]

            reply(unit, outcome).start()

    def finish(unit):
        site, chunk = split(unit)
        slot = lax.rem(unit, 2)

        @pl.loop(0, outcomes)
        def _(outcome):
            reply(unit, outcome).wait_recv()

            @pl.loop(0, rows // band)
            def _(step):
                at = pl.ds(pl.multiple_of(step * band, band), band)
                to = pl.ds(pl.multiple_of(chunk * rows + step * band, band), band)
                total = own[slot, outcome, at, :] + answer[chunk, outcome, at, :].astype(jnp.float32)
                norm = jnp.sum(total * total, axis=1, keepdims=True)
                lane = lax.broadcasted_iota(jnp.int32, (band, norms.shape[1]), 1)
                norms[to, :] = jnp.where(lane == site * outcomes + outcome, norm, norms[to, :])
                selected_ref[to, :] = jnp.where(chosen_ref[site, to, :] == outcome, total, selected_ref[to, :])

        @pl.when(site + 1 < STEPS)
        def _():
            @pl.loop(0, rows // band)
            def _(step):
                to = pl.ds(pl.multiple_of(chunk * rows + step * band, band), band)
                blocks[site + 1, place, to, :] = selected_ref[to, :].astype(blocks.dtype)

    def shuffle(index):
        load(index).wait()

        @pl.when(index + 1 < STEPS * tiles)
        def _():
            load(index + 1).start()

        site, at = lax.div(index, tiles), pl.ds(pl.multiple_of(lax.rem(index, tiles) * tall, tall), tall)
        slot = lax.rem(index, 2)
        for outcome in range(outcomes):
            weights[site, 0, outcome, at, :] = stage[slot, :, outcome, :]
        trade(index).start()

    first = pltpu.make_async_copy(env_ref, blocks.at[0, place], env_sem)
    first.start()
    load(0).start()
    barrier = pltpu.get_barrier_semaphore()
    friends = [{"bond": peers[d]} for d in range(1, bonds)] + [{"samp": sibling}, {"samp": opposite}]
    for friend in friends:
        pl.semaphore_signal(barrier, inc=1, device_id=friend, device_id_type=MESH)
    norms[...] = jnp.zeros_like(norms)
    selected_ref[...] = jnp.zeros_like(selected_ref)
    first.wait()
    pl.semaphore_wait(barrier, len(friends))

    each = -(-STEPS * tiles // (2 * LEAD))

    @pl.loop(0, units + LEAD + 1)
    def _(step):
        now = step - LEAD

        @pl.when((now + 2 >= 0) & (now + 2 < units))
        def _():
            forward_block(now + 2)

        @pl.when((now + 1 >= 0) & (now + 1 < units))
        def _():
            send_foreign(now + 1)

        @pl.when((now >= 0) & (now < units))
        def _():
            multiply(now)

        @pl.when(now >= 1)
        def _():
            finish(now - 1)

        @pl.when(now + 3 < units)
        def _():
            send_blocks(now + 3)

        @pl.loop(0, each)
        def _(turn):
            index = step * each + turn

            @pl.when(index < STEPS * tiles)
            def _():
                shuffle(index)

    for chunk in range(chunks):
        at = pl.ds(chunk * rows, rows)
        gathered[place, :, at] = jnp.transpose(norms[at, :])[: STEPS * outcomes]
    sums = []
    for d in range(1, bonds):
        ref = gathered.at[place]
        sums.append(copy_to(ref, ref, norm_send.at[d - 1], norm_recv.at[d - 1], {"bond": peers[d]}))
    for one in sums:
        one.start()
    for site in range(STEPS):
        trade_all(site).wait_send()

    @pl.loop(0, units)
    def _(unit):
        for d in range(1, bonds):
            hop(unit, d).wait_send()

    for unit in range(units - 2, units):
        cross_part(unit).wait_send()
        for outcome in range(outcomes):
            reply(unit, outcome).wait_send()
    for one in sums:
        one.wait()
    totals_ref[...] = gathered[0] + gathered[1] + gathered[2] + gathered[3]


def sample_sites(env_start, stored_sites, slab_order, chosen):
    groups, bonds = slab_order.shape[1], lax.axis_size("bond")
    mine = lax.axis_index("samp")
    slab, outcomes, width = stored_sites.shape[2:]
    samples = env_start.shape[0]
    rows = samples // PARTS_OF_SITE
    units = STEPS * PARTS_OF_SITE
    tall = min(slab, 128)
    sibling, opposite = mine + 1 - 2 * (mine % 2), (mine + groups // 2) % groups
    opposite_sibling = opposite + 1 - 2 * (opposite % 2)
    wanted = slab_order[:, jnp.stack([mine, sibling, opposite, opposite_sibling])]
    mask = (wanted[:, :, None] == jnp.arange(bonds, dtype=jnp.int32)).astype(jnp.float32).reshape(-1)
    kind = env_start.dtype
    dma = pltpu.SemaphoreType.DMA
    selected, totals = pl.pallas_call(
        functools.partial(sampling_kernel, bonds, groups),
        in_specs=[
            pl.BlockSpec(memory_space=pltpu.SMEM),
            pl.BlockSpec(memory_space=pl.ANY),
            pl.BlockSpec(memory_space=pl.ANY),
            pl.BlockSpec(memory_space=pltpu.VMEM),
        ],
        out_specs=(pl.BlockSpec(memory_space=pltpu.VMEM), pl.BlockSpec(memory_space=pltpu.VMEM)),
        out_shape=(
            jax.ShapeDtypeStruct((samples, width), jnp.float32),
            jax.ShapeDtypeStruct((STEPS * outcomes, samples), jnp.float32),
        ),
        scratch_shapes=[
            pltpu.VMEM((STEPS, 2, outcomes, slab, width), kind),
            pltpu.VMEM((STEPS, bonds, samples, width), kind),
            pltpu.VMEM((PARTS_OF_SITE, 2, rows, width), kind),
            pltpu.VMEM((2, 2, rows, width), kind),
            pltpu.VMEM((2, outcomes, rows, width), kind),
            pltpu.VMEM((PARTS_OF_SITE, outcomes, rows, width), kind),
            pltpu.VMEM((2, outcomes, rows, width), jnp.float32),
            pltpu.VMEM((2, 2 * rows, width), kind),
            pltpu.VMEM((2, tall, outcomes, width), kind),
            pltpu.VMEM((samples, 128), jnp.float32),
            pltpu.VMEM((bonds, STEPS * outcomes, samples), jnp.float32),
            dma,
            dma((2,)),
            dma((STEPS,)),
            dma((STEPS,)),
            dma((units, bonds - 1)),
            dma((units, bonds - 1)),
            dma((units,)),
            dma((units,)),
            dma((units, bonds - 1)),
            dma((units, bonds - 1)),
            dma((units, outcomes)),
            dma((units, outcomes)),
            dma((bonds - 1,)),
            dma((bonds - 1,)),
        ],
        compiler_params=pltpu.CompilerParams(
            collective_id=0, has_side_effects=True, vmem_limit_bytes=67_000_000
        ),
    )(mask, env_start, stored_sites, jnp.transpose(chosen)[:, :, None])
    totals = jnp.transpose(totals).reshape(samples, STEPS, outcomes)
    factor = jnp.ones((samples,), jnp.float32)
    labels = jnp.arange(outcomes, dtype=jnp.int32)
    probabilities = []
    for site in range(STEPS):
        scaled = totals[:, site] * (factor * factor)[:, None]
        probabilities.append(scaled / jnp.sum(scaled, axis=1, keepdims=True))
        hit = chosen[:, site][:, None] == labels[None, :]
        factor = factor * lax.rsqrt(jnp.sum(jnp.where(hit, scaled, 0.0), axis=1) / (width * bonds) + epsilon)
    return jnp.stack(probabilities, axis=1), selected * factor[:, None]


def body(*arrays):
    return compute(*arrays)


def solution(mesh):
    fused = mesh.shape["samp"] == 4 and mesh.shape["bond"] == 4
    return jax.shard_map(
        sample_sites if fused else body,
        mesh=mesh,
        in_specs=(
            P(("parts", "samp"), "bond"),
            P("parts", "samp", None, None, "bond"),
            P("parts", None),
            P(("parts", "samp"), None),
        ),
        out_specs=(P(("parts", "samp"), None, None), P(("parts", "samp"), "bond")),
        check_vma=False,
    )
```

```python
import functools

import jax
import jax.numpy as jnp
from jax import lax
from jax.experimental import pallas as pl
from jax.experimental.pallas import tpu as pltpu
from jax.sharding import PartitionSpec as P


STEPS = 2
CHUNKS = 2
PIECES = 2
epsilon = 1e-06


def tile_of(width):
    return min(width, 256)


def dots(env_ref, weight_refs, outcome):
    total = None
    for part, weight_ref in enumerate(weight_refs):
        term = jnp.dot(env_ref[part], weight_ref[outcome], preferred_element_type=jnp.float32)
        total = term if total is None else total + term
    return total


def product_kernel(count, env_ref, *refs):
    weight_refs, out_ref = refs[:count], refs[count]
    for outcome in range(out_ref.shape[0]):
        out_ref[outcome] = dots(env_ref, weight_refs, outcome).astype(out_ref.dtype)


def product(env, weights, piece, pieces, dtype):
    outcomes, rows, width = weights[0].shape
    count = outcomes // pieces
    samples, tile = env.shape[1], tile_of(width)
    flops = 2 * samples * sum(w.size for w in weights) // pieces
    moved = 2 * sum(w.size for w in weights) // pieces
    return pl.pallas_call(
        functools.partial(product_kernel, len(weights)),
        grid=(width // tile,),
        in_specs=[pl.BlockSpec(env.shape, lambda t: (0, 0, 0))]
        + [pl.BlockSpec((count, rows, tile), lambda t: (piece, 0, t)) for _ in weights],
        out_specs=pl.BlockSpec((count, samples, tile), lambda t: (0, 0, t)),
        out_shape=jax.ShapeDtypeStruct((count, samples, width), dtype),
        cost_estimate=pl.CostEstimate(flops=flops, bytes_accessed=moved, transcendentals=0),
    )(env, *weights)


def finish_kernel(pieces, site, own_ref, chosen_ref, before_ref, *refs):
    other_refs, (totals_ref, selected_ref) = refs[:-2], refs[-2:]
    outcomes = own_ref.shape[0]
    each = outcomes // pieces

    @pl.when(pl.program_id(0) == 0)
    def _():
        totals_ref[...] = before_ref[...]

    lane = lax.broadcasted_iota(jnp.int32, totals_ref.shape, 1)
    selected = None
    added = jnp.zeros(totals_ref.shape, jnp.float32)
    for outcome in range(outcomes):
        total = own_ref[outcome]
        for other_ref in other_refs[outcome // each :: pieces]:
            total = total + other_ref[outcome % each].astype(jnp.float32)
        norm = jnp.sum(total * total, axis=1, keepdims=True)
        added = jnp.where(lane == site * outcomes + outcome, norm, added)
        hit = chosen_ref[...] == outcome
        selected = jnp.where(hit, total, 0.0 if selected is None else selected)
    totals_ref[...] += added
    selected_ref[...] = selected.astype(selected_ref.dtype)


def finish(own, others, chosen, before, site, dtype):
    outcomes, samples, width = own.shape
    tile = tile_of(width)
    pieces = outcomes // others[0].shape[0] if others else 1
    return pl.pallas_call(
        functools.partial(finish_kernel, pieces, site),
        grid=(width // tile,),
        in_specs=[
            pl.BlockSpec((outcomes, samples, tile), lambda t: (0, 0, t)),
            pl.BlockSpec((samples, 1), lambda t: (0, 0)),
            pl.BlockSpec((samples, 128), lambda t: (0, 0)),
        ]
        + [pl.BlockSpec((outcomes // pieces, samples, tile), lambda t: (0, 0, t)) for _ in others],
        out_specs=(
            pl.BlockSpec((samples, 128), lambda t: (0, 0)),
            pl.BlockSpec((samples, tile), lambda t: (0, t)),
        ),
        out_shape=(
            jax.ShapeDtypeStruct((samples, 128), jnp.float32),
            jax.ShapeDtypeStruct((samples, width), dtype),
        ),
        cost_estimate=pl.CostEstimate(
            flops=4 * own.size, bytes_accessed=8 * own.size, transcendentals=0
        ),
    )(own, chosen, before, *others)


def relayout_kernel(stored_ref, _, out_ref):
    for outcome in range(out_ref.shape[0]):
        out_ref[outcome] = stored_ref[0, 0, :, outcome, :]


def relayout(stored_sites, site, after):
    rows, outcomes, width = stored_sites.shape[2:]
    tile = min(rows, 128)
    return pl.pallas_call(
        relayout_kernel,
        grid=(rows // tile,),
        in_specs=[
            pl.BlockSpec((1, 1, tile, outcomes, width), lambda t: (site, 0, t, 0, 0)),
            pl.BlockSpec(memory_space=pl.ANY),
        ],
        out_specs=pl.BlockSpec((outcomes, tile, width), lambda t: (0, t, 0)),
        out_shape=jax.ShapeDtypeStruct((outcomes, rows, width), stored_sites.dtype),
        cost_estimate=pl.CostEstimate(
            flops=0, bytes_accessed=4 * rows * outcomes * width, transcendentals=0
        ),
    )(stored_sites, after)


def pick_kernel(inner, index_ref, *refs):
    pieces, outs = refs[: len(refs) - inner[1]], refs[len(refs) - inner[1] :]
    for target, out_ref in enumerate(outs):
        for part in range(inner[0]):
            for source, piece_ref in enumerate(pieces):

                @pl.when(index_ref[target * inner[0] + part] == source)
                def _():
                    out_ref[part] = piece_ref[...]


def pick_blocks(index, pieces, outer, inner):
    samples, width = pieces[0].shape
    spec = pl.BlockSpec((samples, width), lambda t, index: (0, 0))
    return pl.pallas_call(
        functools.partial(pick_kernel, (inner, outer)),
        grid_spec=pltpu.PrefetchScalarGridSpec(
            num_scalar_prefetch=1,
            grid=(1,),
            in_specs=[spec] * len(pieces),
            out_specs=[pl.BlockSpec((inner, samples, width), lambda t, index: (0, 0, 0))] * outer,
        ),
        out_shape=[jax.ShapeDtypeStruct((inner, samples, width), pieces[0].dtype)] * outer,
        cost_estimate=pl.CostEstimate(
            flops=0, bytes_accessed=2 * samples * width * (len(pieces) + outer * inner), transcendentals=0
        ),
    )(index, *pieces)


def compute(env_start, stored_sites, slab_order, chosen):
    groups = slab_order.shape[1]
    inner = 2 if groups % 2 == 0 else 1
    outer = groups // inner
    bonds = lax.axis_size("bond")
    mine, place = lax.axis_index("samp"), lax.axis_index("bond")
    core, chip = mine % inner, mine // inner
    rows, outcomes, width = stored_sites.shape[2:]
    bond_width = width * bonds
    samples = env_start.shape[0]
    chunks = CHUNKS if samples % (CHUNKS * 16) == 0 else 1
    size = samples // chunks

    def across(value, step):
        return lax.ppermute(
            value, "samp", [(i, ((i // inner + step) % outer) * inner + i % inner) for i in range(groups)]
        )

    def inside(value, step):
        return lax.ppermute(
            value, "samp", [((i // inner) * inner + (i + step) % inner, i) for i in range(groups)]
        )

    def along(value, step):
        return lax.ppermute(value, "bond", [(i, (i + step) % bonds) for i in range(bonds)])

    def load(site, after):
        own = relayout(stored_sites, site, after)
        return [own] + [inside(own, step) for step in range(1, inner)]

    wanted = [
        jnp.stack(
            [
                slab_order[site, ((chip + step) % outer) * inner + (core + part) % inner]
                for step in range(outer)
                for part in range(inner)
            ]
        )
        for site in range(STEPS)
    ]

    def gather(value, site):
        if bonds == groups:
            pieces = [value] + [along(value, step) for step in range(1, bonds)]
            index = (place - wanted[site] + bonds) % bonds
            return lambda: pick_blocks(index, pieces, outer, inner)
        whole = lax.all_gather(value, "bond", axis=1, tiled=True)
        blocks = [
            lax.dynamic_slice_in_dim(whole, wanted[site][i] * rows, rows, axis=1)
            for i in range(groups)
        ]
        return lambda: [
            jnp.stack(blocks[step * inner : (step + 1) * inner]) for step in range(outer)
        ]

    def bond_sum(value):
        if bonds <= 4:
            return sum([along(value, step) for step in range(1, bonds)], value)
        return lax.psum(value, "bond")

    raws = [env_start[c * size : (c + 1) * size] for c in range(chunks)]
    picks = [chosen[c * size : (c + 1) * size] for c in range(chunks)]
    norms = [jnp.zeros((size, 128), jnp.float32)] * chunks

    def fetch(value, site):
        pick = gather(value, site)
        own, *foreign = pick()
        return own, [(i + 1, across(block, i + 1)) for i, block in enumerate(foreign)]

    owns, sents = [], []
    for c in range(chunks):
        own, sent = fetch(raws[c], 0)
        owns.append(own)
        sents.append(sent)
    weights = load(0, norms[0])
    for site in range(STEPS):
        last = site + 1 == STEPS
        answers = []
        for c in range(chunks):
            parts, anchor = [], norms[0]
            for step, foreign in sents[c]:
                for piece in range(PIECES):
                    anchor = product(foreign, weights, piece, PIECES, jnp.bfloat16)
                    parts.append(across(anchor, -step))
            answers.append(parts)
            if c == 0 and not last:
                later = load(site + 1, anchor)
        new_owns, new_sents = [], []
        for c in range(chunks):
            own = product(owns[c], weights, 0, 1, jnp.float32)
            norms[c], raws[c] = finish(
                own,
                answers[c],
                picks[c][:, site : site + 1],
                norms[c],
                site,
                jnp.float32 if last else jnp.bfloat16,
            )
            if not last:
                own, sent = fetch(raws[c], site + 1)
                new_owns.append(own)
                new_sents.append(sent)
        if not last:
            owns, sents, weights = new_owns, new_sents, later
    sums = [bond_sum(norm) for norm in norms]
    totals = [[s[:, site * outcomes : (site + 1) * outcomes] for s in sums] for site in range(STEPS)]
    probabilities, finals = [], []
    labels = jnp.arange(outcomes, dtype=jnp.int32)
    for c in range(chunks):
        factor = jnp.ones((size,), jnp.float32)
        rows_out = []
        for site in range(STEPS):
            scaled = totals[site][c] * (factor * factor)[:, None]
            rows_out.append(scaled / jnp.sum(scaled, axis=1, keepdims=True))
            hit = picks[c][:, site][:, None] == labels[None, :]
            factor = factor * lax.rsqrt(jnp.sum(jnp.where(hit, scaled, 0.0), axis=1) / bond_width + epsilon)
        probabilities.append(jnp.stack(rows_out, axis=1))
        finals.append(raws[c] * factor[:, None])
    return jnp.concatenate(probabilities), jnp.concatenate(finals)


MESH = pl.DeviceIdType.MESH
PARTS_OF_SITE = 4
SHARE = 4
EARLY = 10


def sampling_kernel(
    bonds, groups, order_ref, env_ref, stored_ref, chosen_ref, selected_ref, totals_ref,
    weights, blocks, foreign, picked, partial, answer, own, left, stage, norms, gathered, labels,
    env_sem, stage_sem, weight_send, weight_recv, gather_send, gather_recv, cross_send, cross_recv,
    spread_send, spread_recv, answer_send, answer_recv, norm_send, norm_recv,
):
    mine, place = lax.axis_index("samp"), lax.axis_index("bond")
    core = lax.rem(mine, 2)
    sibling, opposite = mine + 1 - 2 * core, lax.rem(mine + groups // 2, groups)
    peers = (None, place + 1 - 2 * lax.rem(place, 2), lax.rem(place + 2, bonds), bonds - 1 - place)
    middle = lax.div(place + 1, 2) == 1
    outer = lax.div(place + 1, 2) != 1
    outcomes = weights.shape[2]
    width = weights.shape[4]
    chunks = PARTS_OF_SITE
    rows = left.shape[1] // 2
    share = rows // SHARE
    units = STEPS * chunks
    slab = weights.shape[3]
    tall = stage.shape[1]
    tiles = slab // tall
    strip = min(width, 256)
    band = min(rows, 16)

    def copy_to(src, dst, send, recv, where):
        return pltpu.make_async_remote_copy(
            src_ref=src, dst_ref=dst, send_sem=send, recv_sem=recv, device_id=where, device_id_type=MESH
        )

    def split(unit):
        return lax.div(unit, chunks), lax.rem(unit, chunks)

    def spot(chunk):
        return pl.ds(pl.multiple_of(chunk * rows, rows), rows)

    def hop(unit, d):
        site, chunk = split(unit)
        ref = blocks.at[site, place, spot(chunk)]
        return copy_to(ref, ref, gather_send.at[unit, d - 1], gather_recv.at[unit, d - 1], {"bond": peers[d]})

    def relay(unit):
        site, chunk = split(unit)
        ref = blocks.at[site, peers[3], spot(chunk)]
        return copy_to(ref, ref, gather_send.at[unit, 1], gather_recv.at[unit, 1], {"bond": peers[1]})

    half = rows // 2

    def first_hop(part, d):
        ref, to = blocks.at[0, place, pl.ds(part * half, half)], part * units
        return copy_to(ref, ref, gather_send.at[to, d - 1], gather_recv.at[to, d - 1], {"bond": peers[d]})

    def first_relay(part):
        ref, to = blocks.at[0, peers[3], pl.ds(part * half, half)], part * units
        return copy_to(ref, ref, gather_send.at[to, 1], gather_recv.at[to, 1], {"bond": peers[1]})

    def first_cross(part):
        to, at = part * units, pl.ds(part * half, half)
        return copy_to(
            picked.at[0, :, at], foreign.at[0, :, at], cross_send.at[to], cross_recv.at[to], {"samp": opposite}
        )

    def band_of(position):
        return pl.ds(pl.multiple_of(position * share, share), share)

    def cross_part(unit):
        return copy_to(
            picked.at[lax.rem(unit, 2), :, pl.ds(0, share)],
            foreign.at[lax.rem(unit, chunks), :, band_of(lax.rem(place, SHARE))],
            cross_send.at[unit],
            cross_recv.at[unit],
            {"samp": opposite},
        )

    def spread(unit, d):
        ref = foreign.at[lax.rem(unit, chunks), :, band_of(lax.rem(place, SHARE))]
        return copy_to(ref, ref, spread_send.at[unit, d - 1], spread_recv.at[unit, d - 1], {"bond": peers[d]})

    def reply(unit, outcome):
        return copy_to(
            partial.at[lax.rem(unit, 2), outcome],
            answer.at[lax.rem(unit, chunks), outcome],
            answer_send.at[unit, outcome],
            answer_recv.at[unit, outcome],
            {"samp": opposite},
        )

    def load(index):
        return pltpu.make_async_copy(
            stored_ref.at[lax.div(index, tiles), 0, pl.ds(lax.rem(index, tiles) * tall, tall)],
            stage.at[lax.rem(index, 2)],
            stage_sem.at[lax.rem(index, 2)],
        )

    def trade(index):
        site, at = lax.div(index, tiles), pl.ds(pl.multiple_of(lax.rem(index, tiles) * tall, tall), tall)
        return copy_to(
            weights.at[site, 0, :, at],
            weights.at[site, 1, :, at],
            weight_send.at[site],
            weight_recv.at[site],
            {"samp": sibling},
        )

    def trade_all(site):
        return copy_to(
            weights.at[site, 0], weights.at[site, 1], weight_send.at[site], weight_recv.at[site], {"samp": sibling}
        )

    owners = (mine, sibling, opposite, opposite + 1 - 2 * lax.rem(opposite, 2))

    def pick(site, which, at):
        total = None
        for block in range(bonds):
            term = blocks[site, block, at, :].astype(jnp.float32) * jnp.where(order_ref[site, owners[which]] == block, 1.0, 0.0)
            total = term if total is None else total + term
        return total.astype(left.dtype)

    def send_blocks(unit):
        hop(unit, 1).start()
        hop(unit, 3).start()

        @pl.when(outer)
        def _():
            hop(unit, 2).start()

    def forward_block(unit):
        @pl.when(middle)
        def _():
            hop(unit, 3).wait_recv()
            relay(unit).start()

    def send_first(part):
        first_hop(part, 1).start()
        first_hop(part, 3).start()

        @pl.when(outer)
        def _():
            first_hop(part, 2).start()

    def forward_first(part):
        @pl.when(middle)
        def _():
            first_hop(part, 3).wait_recv()
            first_relay(part).start()

    def cross_first(half_at):
        first_hop(half_at, 1).wait_recv()
        first_hop(half_at, 2).wait_recv()

        @pl.when(outer)
        def _():
            first_hop(half_at, 3).wait_recv()

        for part in range(2):

            @pl.loop(0, half // band)
            def _(step):
                at = pl.ds(pl.multiple_of(half_at * half + step * band, band), band)
                picked[0, part, at, :] = pick(0, 2 + part, at)

        first_cross(half_at).start()

    def send_foreign(unit):
        site, chunk = split(unit)
        hop(unit, 1).wait_recv()
        hop(unit, 2).wait_recv()

        @pl.when(outer)
        def _():
            hop(unit, 3).wait_recv()

        slot = lax.rem(unit, 2)

        @pl.when(unit == 2)
        def _():
            for part in range(2):
                first_cross(part).wait_send()

        @pl.when(unit > 2)
        def _():
            cross_part(unit - 2).wait_send()

        at = pl.multiple_of(chunk * rows + lax.rem(place, SHARE) * share, share)
        for part in range(2):
            picked[slot, part, pl.ds(0, share), :] = pick(site, 2 + part, pl.ds(at, share))
        cross_part(unit).start()

    def spread_foreign(unit):
        cross_part(unit).wait_recv()
        spread(unit, 1).start()
        spread(unit, 3).start()

        @pl.when(outer)
        def _():
            spread(unit, 2).start()

    def forward_foreign(unit):
        @pl.when(middle)
        def _():
            spread(unit, 3).wait_recv()
            ref = foreign.at[lax.rem(unit, chunks), :, band_of(peers[3])]
            copy_to(ref, ref, spread_send.at[unit, 1], spread_recv.at[unit, 1], {"bond": peers[1]}).start()

    def multiply(unit):
        site, chunk = split(unit)
        slot = lax.rem(unit, 2)

        for part in range(2):

            @pl.loop(0, rows // band)
            def _(step):
                at = pl.multiple_of(step * band, band)
                left[part, pl.ds(rows + at, band), :] = pick(site, part, pl.ds(chunk * rows + at, band))

        @pl.when(unit == 0)
        def _():
            for part in range(2):
                first_cross(part).wait_recv()

        @pl.when(unit > 0)
        def _():
            spread(unit, 1).wait_recv()
            spread(unit, 2).wait_recv()

            @pl.when(outer)
            def _():
                spread(unit, 3).wait_recv()

            for d in range(1, SHARE):
                spread(unit, d).wait_send()

        for part in range(2):
            left[part, pl.ds(0, rows), :] = foreign[chunk, part]

        @pl.when(chunk == 0)
        def _():
            trade_all(site).wait_recv()

        @pl.loop(0, outcomes)
        def _(outcome):
            @pl.when((outcome == outcomes // 2) & (unit == 0))
            def _():
                send_foreign(unit + 1)

            @pl.when((outcome == outcomes // 2) & (unit > 0) & (unit + 1 < units))
            def _():
                spread_foreign(unit + 1)

            @pl.when(unit >= 2)
            def _():
                reply(unit - 2, outcome).wait_send()

            @pl.loop(0, width // strip)
            def _(step):
                at = pl.ds(pl.multiple_of(step * strip, strip), strip)
                total = jnp.dot(left[0], weights[site, 0, outcome, :, at], preferred_element_type=jnp.float32)
                total = total + jnp.dot(left[1], weights[site, 1, outcome, :, at], preferred_element_type=jnp.float32)
                partial[slot, outcome, :, at] = total[:rows].astype(partial.dtype)
                own[slot, outcome, :, at] = total[rows:]

            reply(unit, outcome).start()

    def finish(unit):
        site, chunk = split(unit)
        slot = lax.rem(unit, 2)

        @pl.loop(0, outcomes)
        def _(outcome):
            reply(unit, outcome).wait_recv()

            @pl.loop(0, rows // band)
            def _(step):
                at = pl.ds(pl.multiple_of(step * band, band), band)
                to = pl.ds(pl.multiple_of(chunk * rows + step * band, band), band)
                total = own[slot, outcome, at, :] + answer[chunk, outcome, at, :].astype(jnp.float32)
                norm = jnp.sum(total * total, axis=1, keepdims=True)
                lane = lax.broadcasted_iota(jnp.int32, (band, norms.shape[1]), 1)
                norms[to, :] = jnp.where(lane == site * outcomes + outcome, norm, norms[to, :])
                selected_ref[to, :] = jnp.where(labels[site, to, :1] == outcome, total, selected_ref[to, :])

        @pl.when(site + 1 < STEPS)
        def _():
            @pl.loop(0, rows // band)
            def _(step):
                to = pl.ds(pl.multiple_of(chunk * rows + step * band, band), band)
                blocks[site + 1, place, to, :] = selected_ref[to, :].astype(blocks.dtype)

    def shuffle(index):
        load(index).wait()

        @pl.when(index + 1 < STEPS * tiles)
        def _():
            load(index + 1).start()

        site, at = lax.div(index, tiles), pl.ds(pl.multiple_of(lax.rem(index, tiles) * tall, tall), tall)
        slot = lax.rem(index, 2)
        for outcome in range(outcomes):
            weights[site, 0, outcome, at, :] = stage[slot, :, outcome, :]
        trade(index).start()

    first = pltpu.make_async_copy(env_ref, blocks.at[0, place], env_sem)
    first.start()
    load(0).start()
    barrier = pltpu.get_barrier_semaphore()
    friends = [{"bond": peers[d]} for d in range(1, bonds)] + [{"samp": sibling}, {"samp": opposite}]
    for friend in friends:
        pl.semaphore_signal(barrier, inc=1, device_id=friend, device_id_type=MESH)
    norms[...] = jnp.zeros_like(norms)
    first.wait()
    pl.semaphore_wait(barrier, len(friends))

    def shuffle_some(start, stop):
        @pl.loop(start, stop)
        def _(index):
            @pl.when(index < STEPS * tiles)
            def _():
                shuffle(index)

    send_first(0)
    shuffle_some(0, 1)
    forward_first(0)
    send_first(1)
    shuffle_some(1, 3)
    forward_first(1)
    send_blocks(1)
    shuffle_some(3, 5)
    cross_first(0)
    shuffle_some(5, 7)
    cross_first(1)
    shuffle_some(7, EARLY)
    selected_ref[...] = jnp.zeros_like(selected_ref)
    for site in range(STEPS):
        for chunk in range(chunks):
            at = pl.ds(chunk * rows, rows)
            wide = jnp.broadcast_to(chosen_ref[site : site + 1, at], (128, rows))
            labels[site, at, :] = jnp.transpose(wide)
    forward_block(1)
    send_blocks(2)

    @pl.loop(0, units + 1)
    def _(now):
        @pl.when((now > 0) & (now + 1 < units))
        def _():
            send_foreign(now + 1)

        @pl.when(now < units)
        def _():
            multiply(now)

        @pl.when(now >= 1)
        def _():
            finish(now - 1)

        @pl.when(now == 0)
        def _():
            spread_foreign(now + 1)

        @pl.when(now + 2 < units)
        def _():
            forward_block(now + 2)

        @pl.when(now + 1 < units)
        def _():
            forward_foreign(now + 1)

        @pl.when(now + 3 < units)
        def _():
            send_blocks(now + 3)

        shuffle_some(EARLY + 2 * now, EARLY + 2 * now + 2)

    for chunk in range(chunks):
        at = pl.ds(chunk * rows, rows)
        gathered[place, :, at] = jnp.transpose(norms[at, :])[: STEPS * outcomes]
    sums = []
    for d in range(1, bonds):
        ref = gathered.at[place]
        sums.append(copy_to(ref, ref, norm_send.at[d - 1], norm_recv.at[d - 1], {"bond": peers[d]}))
    for one in sums:
        one.start()
    for site in range(STEPS):
        trade_all(site).wait_send()

    @pl.loop(1, units)
    def _(unit):
        for d in range(1, bonds):
            hop(unit, d).wait_send()

    for part in range(2):
        for d in range(1, bonds):
            first_hop(part, d).wait_send()

    for unit in range(units - 2, units):
        cross_part(unit).wait_send()
        for outcome in range(outcomes):
            reply(unit, outcome).wait_send()
    for one in sums:
        one.wait()
    totals_ref[...] = gathered[0] + gathered[1] + gathered[2] + gathered[3]


def sample_sites(env_start, stored_sites, slab_order, chosen):
    groups, bonds = slab_order.shape[1], lax.axis_size("bond")
    slab, outcomes, width = stored_sites.shape[2:]
    samples = env_start.shape[0]
    rows = samples // PARTS_OF_SITE
    units = STEPS * PARTS_OF_SITE
    tall = min(slab, 128)
    kind = env_start.dtype
    dma = pltpu.SemaphoreType.DMA
    selected, totals = pl.pallas_call(
        functools.partial(sampling_kernel, bonds, groups),
        in_specs=[
            pl.BlockSpec(memory_space=pltpu.SMEM),
            pl.BlockSpec(memory_space=pl.ANY),
            pl.BlockSpec(memory_space=pl.ANY),
            pl.BlockSpec(memory_space=pltpu.VMEM),
        ],
        out_specs=(pl.BlockSpec(memory_space=pltpu.VMEM), pl.BlockSpec(memory_space=pltpu.VMEM)),
        out_shape=(
            jax.ShapeDtypeStruct((samples, width), jnp.float32),
            jax.ShapeDtypeStruct((STEPS * outcomes, samples), jnp.float32),
        ),
        scratch_shapes=[
            pltpu.VMEM((STEPS, 2, outcomes, slab, width), kind),
            pltpu.VMEM((STEPS, bonds, samples, width), kind),
            pltpu.VMEM((PARTS_OF_SITE, 2, rows, width), kind),
            pltpu.VMEM((2, 2, rows, width), kind),
            pltpu.VMEM((2, outcomes, rows, width), kind),
            pltpu.VMEM((PARTS_OF_SITE, outcomes, rows, width), kind),
            pltpu.VMEM((2, outcomes, rows, width), jnp.float32),
            pltpu.VMEM((2, 2 * rows, width), kind),
            pltpu.VMEM((2, tall, outcomes, width), kind),
            pltpu.VMEM((samples, 128), jnp.float32),
            pltpu.VMEM((bonds, STEPS * outcomes, samples), jnp.float32),
            pltpu.VMEM((STEPS, samples, 128), jnp.int32),
            dma,
            dma((2,)),
            dma((STEPS,)),
            dma((STEPS,)),
            dma((units + 1, bonds - 1)),
            dma((units + 1, bonds - 1)),
            dma((units + 1,)),
            dma((units + 1,)),
            dma((units, bonds - 1)),
            dma((units, bonds - 1)),
            dma((units, outcomes)),
            dma((units, outcomes)),
            dma((bonds - 1,)),
            dma((bonds - 1,)),
        ],
        compiler_params=pltpu.CompilerParams(
            collective_id=0, has_side_effects=True, vmem_limit_bytes=67_000_000
        ),
    )(slab_order, env_start, stored_sites, jnp.transpose(chosen))
    totals = jnp.transpose(totals).reshape(samples, STEPS, outcomes)
    factor = jnp.ones((samples,), jnp.float32)
    labels = jnp.arange(outcomes, dtype=jnp.int32)
    probabilities = []
    for site in range(STEPS):
        scaled = totals[:, site] * (factor * factor)[:, None]
        probabilities.append(scaled / jnp.sum(scaled, axis=1, keepdims=True))
        hit = chosen[:, site][:, None] == labels[None, :]
        factor = factor * lax.rsqrt(jnp.sum(jnp.where(hit, scaled, 0.0), axis=1) / (width * bonds) + epsilon)
    return jnp.stack(probabilities, axis=1), selected * factor[:, None]


def body(*arrays):
    return compute(*arrays)


def solution(mesh):
    fused = mesh.shape["samp"] == 4 and mesh.shape["bond"] == 4
    return jax.shard_map(
        sample_sites if fused else body,
        mesh=mesh,
        in_specs=(
            P(("parts", "samp"), "bond"),
            P("parts", "samp", None, None, "bond"),
            P("parts", None),
            P(("parts", "samp"), None),
        ),
        out_specs=(P(("parts", "samp"), None, None), P(("parts", "samp"), "bond")),
        check_vma=False,
    )
```

```python
import functools

import jax
import jax.numpy as jnp
from jax import lax
from jax.experimental import pallas as pl
from jax.experimental.pallas import tpu as pltpu
from jax.sharding import PartitionSpec as P


STEPS = 2
CHUNKS = 2
PIECES = 2
epsilon = 1e-06


def tile_of(width):
    return min(width, 256)


def dots(env_ref, weight_refs, outcome):
    total = None
    for part, weight_ref in enumerate(weight_refs):
        term = jnp.dot(env_ref[part], weight_ref[outcome], preferred_element_type=jnp.float32)
        total = term if total is None else total + term
    return total


def product_kernel(count, env_ref, *refs):
    weight_refs, out_ref = refs[:count], refs[count]
    for outcome in range(out_ref.shape[0]):
        out_ref[outcome] = dots(env_ref, weight_refs, outcome).astype(out_ref.dtype)


def product(env, weights, piece, pieces, dtype):
    outcomes, rows, width = weights[0].shape
    count = outcomes // pieces
    samples, tile = env.shape[1], tile_of(width)
    flops = 2 * samples * sum(w.size for w in weights) // pieces
    moved = 2 * sum(w.size for w in weights) // pieces
    return pl.pallas_call(
        functools.partial(product_kernel, len(weights)),
        grid=(width // tile,),
        in_specs=[pl.BlockSpec(env.shape, lambda t: (0, 0, 0))]
        + [pl.BlockSpec((count, rows, tile), lambda t: (piece, 0, t)) for _ in weights],
        out_specs=pl.BlockSpec((count, samples, tile), lambda t: (0, 0, t)),
        out_shape=jax.ShapeDtypeStruct((count, samples, width), dtype),
        cost_estimate=pl.CostEstimate(flops=flops, bytes_accessed=moved, transcendentals=0),
    )(env, *weights)


def finish_kernel(pieces, site, own_ref, chosen_ref, before_ref, *refs):
    other_refs, (totals_ref, selected_ref) = refs[:-2], refs[-2:]
    outcomes = own_ref.shape[0]
    each = outcomes // pieces

    @pl.when(pl.program_id(0) == 0)
    def _():
        totals_ref[...] = before_ref[...]

    lane = lax.broadcasted_iota(jnp.int32, totals_ref.shape, 1)
    selected = None
    added = jnp.zeros(totals_ref.shape, jnp.float32)
    for outcome in range(outcomes):
        total = own_ref[outcome]
        for other_ref in other_refs[outcome // each :: pieces]:
            total = total + other_ref[outcome % each].astype(jnp.float32)
        norm = jnp.sum(total * total, axis=1, keepdims=True)
        added = jnp.where(lane == site * outcomes + outcome, norm, added)
        hit = chosen_ref[...] == outcome
        selected = jnp.where(hit, total, 0.0 if selected is None else selected)
    totals_ref[...] += added
    selected_ref[...] = selected.astype(selected_ref.dtype)


def finish(own, others, chosen, before, site, dtype):
    outcomes, samples, width = own.shape
    tile = tile_of(width)
    pieces = outcomes // others[0].shape[0] if others else 1
    return pl.pallas_call(
        functools.partial(finish_kernel, pieces, site),
        grid=(width // tile,),
        in_specs=[
            pl.BlockSpec((outcomes, samples, tile), lambda t: (0, 0, t)),
            pl.BlockSpec((samples, 1), lambda t: (0, 0)),
            pl.BlockSpec((samples, 128), lambda t: (0, 0)),
        ]
        + [pl.BlockSpec((outcomes // pieces, samples, tile), lambda t: (0, 0, t)) for _ in others],
        out_specs=(
            pl.BlockSpec((samples, 128), lambda t: (0, 0)),
            pl.BlockSpec((samples, tile), lambda t: (0, t)),
        ),
        out_shape=(
            jax.ShapeDtypeStruct((samples, 128), jnp.float32),
            jax.ShapeDtypeStruct((samples, width), dtype),
        ),
        cost_estimate=pl.CostEstimate(
            flops=4 * own.size, bytes_accessed=8 * own.size, transcendentals=0
        ),
    )(own, chosen, before, *others)


def relayout_kernel(stored_ref, _, out_ref):
    for outcome in range(out_ref.shape[0]):
        out_ref[outcome] = stored_ref[0, 0, :, outcome, :]


def relayout(stored_sites, site, after):
    rows, outcomes, width = stored_sites.shape[2:]
    tile = min(rows, 128)
    return pl.pallas_call(
        relayout_kernel,
        grid=(rows // tile,),
        in_specs=[
            pl.BlockSpec((1, 1, tile, outcomes, width), lambda t: (site, 0, t, 0, 0)),
            pl.BlockSpec(memory_space=pl.ANY),
        ],
        out_specs=pl.BlockSpec((outcomes, tile, width), lambda t: (0, t, 0)),
        out_shape=jax.ShapeDtypeStruct((outcomes, rows, width), stored_sites.dtype),
        cost_estimate=pl.CostEstimate(
            flops=0, bytes_accessed=4 * rows * outcomes * width, transcendentals=0
        ),
    )(stored_sites, after)


def pick_kernel(inner, index_ref, *refs):
    pieces, outs = refs[: len(refs) - inner[1]], refs[len(refs) - inner[1] :]
    for target, out_ref in enumerate(outs):
        for part in range(inner[0]):
            for source, piece_ref in enumerate(pieces):

                @pl.when(index_ref[target * inner[0] + part] == source)
                def _():
                    out_ref[part] = piece_ref[...]


def pick_blocks(index, pieces, outer, inner):
    samples, width = pieces[0].shape
    spec = pl.BlockSpec((samples, width), lambda t, index: (0, 0))
    return pl.pallas_call(
        functools.partial(pick_kernel, (inner, outer)),
        grid_spec=pltpu.PrefetchScalarGridSpec(
            num_scalar_prefetch=1,
            grid=(1,),
            in_specs=[spec] * len(pieces),
            out_specs=[pl.BlockSpec((inner, samples, width), lambda t, index: (0, 0, 0))] * outer,
        ),
        out_shape=[jax.ShapeDtypeStruct((inner, samples, width), pieces[0].dtype)] * outer,
        cost_estimate=pl.CostEstimate(
            flops=0, bytes_accessed=2 * samples * width * (len(pieces) + outer * inner), transcendentals=0
        ),
    )(index, *pieces)


def compute(env_start, stored_sites, slab_order, chosen):
    groups = slab_order.shape[1]
    inner = 2 if groups % 2 == 0 else 1
    outer = groups // inner
    bonds = lax.axis_size("bond")
    mine, place = lax.axis_index("samp"), lax.axis_index("bond")
    core, chip = mine % inner, mine // inner
    rows, outcomes, width = stored_sites.shape[2:]
    bond_width = width * bonds
    samples = env_start.shape[0]
    chunks = CHUNKS if samples % (CHUNKS * 16) == 0 else 1
    size = samples // chunks

    def across(value, step):
        return lax.ppermute(
            value, "samp", [(i, ((i // inner + step) % outer) * inner + i % inner) for i in range(groups)]
        )

    def inside(value, step):
        return lax.ppermute(
            value, "samp", [((i // inner) * inner + (i + step) % inner, i) for i in range(groups)]
        )

    def along(value, step):
        return lax.ppermute(value, "bond", [(i, (i + step) % bonds) for i in range(bonds)])

    def load(site, after):
        own = relayout(stored_sites, site, after)
        return [own] + [inside(own, step) for step in range(1, inner)]

    wanted = [
        jnp.stack(
            [
                slab_order[site, ((chip + step) % outer) * inner + (core + part) % inner]
                for step in range(outer)
                for part in range(inner)
            ]
        )
        for site in range(STEPS)
    ]

    def gather(value, site):
        if bonds == groups:
            pieces = [value] + [along(value, step) for step in range(1, bonds)]
            index = (place - wanted[site] + bonds) % bonds
            return lambda: pick_blocks(index, pieces, outer, inner)
        whole = lax.all_gather(value, "bond", axis=1, tiled=True)
        blocks = [
            lax.dynamic_slice_in_dim(whole, wanted[site][i] * rows, rows, axis=1)
            for i in range(groups)
        ]
        return lambda: [
            jnp.stack(blocks[step * inner : (step + 1) * inner]) for step in range(outer)
        ]

    def bond_sum(value):
        if bonds <= 4:
            return sum([along(value, step) for step in range(1, bonds)], value)
        return lax.psum(value, "bond")

    raws = [env_start[c * size : (c + 1) * size] for c in range(chunks)]
    picks = [chosen[c * size : (c + 1) * size] for c in range(chunks)]
    norms = [jnp.zeros((size, 128), jnp.float32)] * chunks

    def fetch(value, site):
        pick = gather(value, site)
        own, *foreign = pick()
        return own, [(i + 1, across(block, i + 1)) for i, block in enumerate(foreign)]

    owns, sents = [], []
    for c in range(chunks):
        own, sent = fetch(raws[c], 0)
        owns.append(own)
        sents.append(sent)
    weights = load(0, norms[0])
    for site in range(STEPS):
        last = site + 1 == STEPS
        answers = []
        for c in range(chunks):
            parts, anchor = [], norms[0]
            for step, foreign in sents[c]:
                for piece in range(PIECES):
                    anchor = product(foreign, weights, piece, PIECES, jnp.bfloat16)
                    parts.append(across(anchor, -step))
            answers.append(parts)
            if c == 0 and not last:
                later = load(site + 1, anchor)
        new_owns, new_sents = [], []
        for c in range(chunks):
            own = product(owns[c], weights, 0, 1, jnp.float32)
            norms[c], raws[c] = finish(
                own,
                answers[c],
                picks[c][:, site : site + 1],
                norms[c],
                site,
                jnp.float32 if last else jnp.bfloat16,
            )
            if not last:
                own, sent = fetch(raws[c], site + 1)
                new_owns.append(own)
                new_sents.append(sent)
        if not last:
            owns, sents, weights = new_owns, new_sents, later
    sums = [bond_sum(norm) for norm in norms]
    totals = [[s[:, site * outcomes : (site + 1) * outcomes] for s in sums] for site in range(STEPS)]
    probabilities, finals = [], []
    labels = jnp.arange(outcomes, dtype=jnp.int32)
    for c in range(chunks):
        factor = jnp.ones((size,), jnp.float32)
        rows_out = []
        for site in range(STEPS):
            scaled = totals[site][c] * (factor * factor)[:, None]
            rows_out.append(scaled / jnp.sum(scaled, axis=1, keepdims=True))
            hit = picks[c][:, site][:, None] == labels[None, :]
            factor = factor * lax.rsqrt(jnp.sum(jnp.where(hit, scaled, 0.0), axis=1) / bond_width + epsilon)
        probabilities.append(jnp.stack(rows_out, axis=1))
        finals.append(raws[c] * factor[:, None])
    return jnp.concatenate(probabilities), jnp.concatenate(finals)


MESH = pl.DeviceIdType.MESH
PARTS_OF_SITE = 4
SHARE = 4
EARLY = 9


def sampling_kernel(
    bonds, groups, order_ref, env_ref, stored_ref, chosen_ref, result_ref, totals_ref,
    weights, blocks, foreign, picked, partial, answer, own, left, stage, norms, gathered, labels, selected_ref,
    env_sem, stage_sem, weight_send, weight_recv, gather_send, gather_recv, cross_send, cross_recv,
    spread_send, spread_recv, answer_send, answer_recv, norm_send, norm_recv, result_sem,
):
    mine, place = lax.axis_index("samp"), lax.axis_index("bond")
    core = lax.rem(mine, 2)
    sibling, opposite = mine + 1 - 2 * core, lax.rem(mine + groups // 2, groups)
    peers = (None, place + 1 - 2 * lax.rem(place, 2), lax.rem(place + 2, bonds), bonds - 1 - place)
    middle = lax.div(place + 1, 2) == 1
    outer = lax.div(place + 1, 2) != 1
    outcomes = weights.shape[2]
    width = weights.shape[4]
    chunks = PARTS_OF_SITE
    rows = left.shape[1] // 2
    share = rows // SHARE
    units = STEPS * chunks
    wide = stage.shape[3]
    tiles = width // wide
    strips, strip = own.shape[1], own.shape[4]
    per = strip // wide
    band = min(rows, 16)

    def copy_to(src, dst, send, recv, where):
        return pltpu.make_async_remote_copy(
            src_ref=src, dst_ref=dst, send_sem=send, recv_sem=recv, device_id=where, device_id_type=MESH
        )

    def split(unit):
        return lax.div(unit, chunks), lax.rem(unit, chunks)

    def spot(chunk):
        return pl.ds(pl.multiple_of(chunk * rows, rows), rows)

    def hop(unit, d):
        site, chunk = split(unit)
        ref = blocks.at[site, place, spot(chunk)]
        return copy_to(ref, ref, gather_send.at[unit, d - 1], gather_recv.at[unit, d - 1], {"bond": peers[d]})

    def relay(unit):
        site, chunk = split(unit)
        ref = blocks.at[site, peers[3], spot(chunk)]
        return copy_to(ref, ref, gather_send.at[unit, 1], gather_recv.at[unit, 1], {"bond": peers[1]})

    half = rows // 2

    def first_hop(part, d):
        ref, to = blocks.at[0, place, pl.ds(part * half, half)], part * units
        return copy_to(ref, ref, gather_send.at[to, d - 1], gather_recv.at[to, d - 1], {"bond": peers[d]})

    def first_relay(part):
        ref, to = blocks.at[0, peers[3], pl.ds(part * half, half)], part * units
        return copy_to(ref, ref, gather_send.at[to, 1], gather_recv.at[to, 1], {"bond": peers[1]})

    def first_cross(part):
        to, at = part * units, pl.ds(part * half, half)
        return copy_to(
            picked.at[0, :, at], foreign.at[0, :, at], cross_send.at[to], cross_recv.at[to], {"samp": opposite}
        )

    def band_of(position):
        return pl.ds(pl.multiple_of(position * share, share), share)

    def cross_part(unit):
        return copy_to(
            picked.at[lax.rem(unit, 2), :, pl.ds(0, share)],
            foreign.at[lax.rem(unit, chunks), :, band_of(lax.rem(place, SHARE))],
            cross_send.at[unit],
            cross_recv.at[unit],
            {"samp": opposite},
        )

    def spread(unit, d):
        ref = foreign.at[lax.rem(unit, chunks), :, band_of(lax.rem(place, SHARE))]
        return copy_to(ref, ref, spread_send.at[unit, d - 1], spread_recv.at[unit, d - 1], {"bond": peers[d]})

    def reply(unit, at):
        return copy_to(
            partial.at[lax.rem(unit, 2), at],
            answer.at[lax.rem(unit, chunks), at],
            answer_send.at[unit, at],
            answer_recv.at[unit, at],
            {"samp": opposite},
        )

    def load(index):
        return pltpu.make_async_copy(
            stored_ref.at[lax.div(index, tiles), 0, :, :, pl.ds(pl.multiple_of(lax.rem(index, tiles) * wide, wide), wide)],
            stage.at[lax.rem(index, 2)],
            stage_sem.at[lax.rem(index, 2)],
        )

    def trade(index):
        site, tile = lax.div(index, tiles), lax.rem(index, tiles)
        at = pl.ds(pl.multiple_of(tile * wide, wide), wide)
        return copy_to(
            weights.at[site, 0, :, :, at],
            weights.at[site, 1, :, :, at],
            weight_send.at[site, lax.div(tile, per)],
            weight_recv.at[site, lax.div(tile, per)],
            {"samp": sibling},
        )

    def columns(at):
        return pl.ds(pl.multiple_of(at * strip, strip), strip)

    def trade_all(site, at):
        return copy_to(
            weights.at[site, 0, :, :, columns(at)],
            weights.at[site, 1, :, :, columns(at)],
            weight_send.at[site, at],
            weight_recv.at[site, at],
            {"samp": sibling},
        )

    owners = (mine, sibling, opposite, opposite + 1 - 2 * lax.rem(opposite, 2))

    def pick(site, which, at):
        total = None
        for block in range(bonds):
            term = blocks[site, block, at, :].astype(jnp.float32) * jnp.where(order_ref[site, owners[which]] == block, 1.0, 0.0)
            total = term if total is None else total + term
        return total.astype(left.dtype)

    def send_blocks(unit):
        hop(unit, 1).start()
        hop(unit, 3).start()

        @pl.when(outer)
        def _():
            hop(unit, 2).start()

    def forward_block(unit):
        @pl.when(middle)
        def _():
            hop(unit, 3).wait_recv()
            relay(unit).start()

    def send_first(part):
        first_hop(part, 1).start()
        first_hop(part, 3).start()

        @pl.when(outer)
        def _():
            first_hop(part, 2).start()

    def forward_first(part):
        @pl.when(middle)
        def _():
            first_hop(part, 3).wait_recv()
            first_relay(part).start()

    def cross_first(half_at):
        first_hop(half_at, 1).wait_recv()
        first_hop(half_at, 2).wait_recv()

        @pl.when(outer)
        def _():
            first_hop(half_at, 3).wait_recv()

        for part in range(2):

            @pl.loop(0, half // band)
            def _(step):
                at = pl.ds(pl.multiple_of(half_at * half + step * band, band), band)
                picked[0, part, at, :] = pick(0, 2 + part, at)

        first_cross(half_at).start()

    def send_foreign(unit):
        site, chunk = split(unit)
        hop(unit, 1).wait_recv()
        hop(unit, 2).wait_recv()

        @pl.when(outer)
        def _():
            hop(unit, 3).wait_recv()

        slot = lax.rem(unit, 2)

        @pl.when(unit == 2)
        def _():
            for part in range(2):
                first_cross(part).wait_send()

        @pl.when(unit > 2)
        def _():
            cross_part(unit - 2).wait_send()

        at = pl.multiple_of(chunk * rows + lax.rem(place, SHARE) * share, share)
        for part in range(2):
            picked[slot, part, pl.ds(0, share), :] = pick(site, 2 + part, pl.ds(at, share))
        cross_part(unit).start()

    def spread_foreign(unit):
        cross_part(unit).wait_recv()
        spread(unit, 1).start()
        spread(unit, 3).start()

        @pl.when(outer)
        def _():
            spread(unit, 2).start()

    def forward_foreign(unit):
        @pl.when(middle)
        def _():
            spread(unit, 3).wait_recv()
            ref = foreign.at[lax.rem(unit, chunks), :, band_of(peers[3])]
            copy_to(ref, ref, spread_send.at[unit, 1], spread_recv.at[unit, 1], {"bond": peers[1]}).start()

    def multiply(unit):
        site, chunk = split(unit)
        slot = lax.rem(unit, 2)

        for part in range(2):

            @pl.loop(0, rows // band)
            def _(step):
                at = pl.multiple_of(step * band, band)
                left[part, pl.ds(rows + at, band), :] = pick(site, part, pl.ds(chunk * rows + at, band))

        @pl.when(unit == 0)
        def _():
            for part in range(2):
                first_cross(part).wait_recv()

        @pl.when(unit > 0)
        def _():
            spread(unit, 1).wait_recv()
            spread(unit, 2).wait_recv()

            @pl.when(outer)
            def _():
                spread(unit, 3).wait_recv()

            for d in range(1, SHARE):
                spread(unit, d).wait_send()

        for part in range(2):
            left[part, pl.ds(0, rows), :] = foreign[chunk, part]

        @pl.loop(0, strips)
        def _(at):
            @pl.when((at == strips // 2) & (unit == 0))
            def _():
                send_foreign(unit + 1)

            @pl.when((at == strips // 2) & (unit > 0) & (unit + 1 < units))
            def _():
                spread_foreign(unit + 1)

            @pl.when(chunk == 0)
            def _():
                trade_all(site, at).wait_recv()

            @pl.when(unit >= 2)
            def _():
                reply(unit - 2, at).wait_send()

            @pl.loop(0, outcomes)
            def _(outcome):
                total = jnp.dot(left[0], weights[site, 0, outcome, :, columns(at)], preferred_element_type=jnp.float32)
                total = total + jnp.dot(
                    left[1], weights[site, 1, outcome, :, columns(at)], preferred_element_type=jnp.float32
                )
                partial[slot, at, outcome] = total[:rows].astype(partial.dtype)
                own[slot, at, outcome] = total[rows:]

            reply(unit, at).start()

    def store(chunk):
        return pltpu.make_async_copy(
            selected_ref.at[spot(chunk)], result_ref.at[spot(chunk)], result_sem.at[chunk]
        )

    def total_up(chunk, d):
        ref = gathered.at[place, :, spot(chunk)]
        return copy_to(ref, ref, norm_send.at[chunk, d - 1], norm_recv.at[chunk, d - 1], {"bond": peers[d]})

    def finish(unit):
        site, chunk = split(unit)
        slot = lax.rem(unit, 2)

        @pl.loop(0, strips)
        def _(at):
            reply(unit, at).wait_recv()

            @pl.loop(0, rows // band)
            def _(step):
                here = pl.ds(pl.multiple_of(step * band, band), band)
                to = pl.ds(pl.multiple_of(chunk * rows + step * band, band), band)
                lane = lax.broadcasted_iota(jnp.int32, (band, norms.shape[1]), 1)
                label = labels[site, to, :1]
                added, chosen = norms[to, :], None
                for outcome in range(outcomes):
                    total = own[slot, at, outcome, here, :] + answer[chunk, at, outcome, here, :].astype(jnp.float32)
                    norm = jnp.sum(total * total, axis=1, keepdims=True)
                    added = added + jnp.where(lane == site * outcomes + outcome, norm, 0.0)
                    chosen = total if chosen is None else jnp.where(label == outcome, total, chosen)
                norms[to, :] = added

                @pl.when(site + 1 < STEPS)
                def _():
                    blocks[site + 1, place, to, columns(at)] = chosen.astype(blocks.dtype)

                @pl.when(site + 1 == STEPS)
                def _():
                    selected_ref[to, columns(at)] = chosen

        @pl.when(site + 1 == STEPS)
        def _():
            store(chunk).start()
            gathered[place, :, spot(chunk)] = jnp.transpose(norms[spot(chunk), :])[: STEPS * outcomes]
            for d in range(1, bonds):
                total_up(chunk, d).start()

    def shuffle(index):
        load(index).wait()

        @pl.when(index + 1 < STEPS * tiles)
        def _():
            load(index + 1).start()

        site, at = lax.div(index, tiles), pl.ds(pl.multiple_of(lax.rem(index, tiles) * wide, wide), wide)
        slot = lax.rem(index, 2)
        for outcome in range(outcomes):
            weights[site, 0, outcome, :, at] = stage[slot, :, outcome, :]
        trade(index).start()

    first = pltpu.make_async_copy(env_ref, blocks.at[0, place], env_sem)
    first.start()
    load(0).start()
    barrier = pltpu.get_barrier_semaphore()
    friends = [{"bond": peers[d]} for d in range(1, bonds)] + [{"samp": sibling}, {"samp": opposite}]
    for friend in friends:
        pl.semaphore_signal(barrier, inc=1, device_id=friend, device_id_type=MESH)
    norms[...] = jnp.zeros_like(norms)
    first.wait()
    pl.semaphore_wait(barrier, len(friends))

    def shuffle_some(start, stop):
        @pl.loop(start, stop)
        def _(index):
            @pl.when(index < STEPS * tiles)
            def _():
                shuffle(index)

    send_first(0)
    shuffle_some(0, 1)
    forward_first(0)
    send_first(1)
    shuffle_some(1, 3)
    forward_first(1)
    send_blocks(1)
    shuffle_some(3, 5)
    cross_first(0)
    shuffle_some(5, 7)
    cross_first(1)
    shuffle_some(7, EARLY)
    for site in range(STEPS):
        for chunk in range(chunks):
            at = pl.ds(chunk * rows, rows)
            spreaded = jnp.broadcast_to(chosen_ref[site : site + 1, at], (128, rows))
            labels[site, at, :] = jnp.transpose(spreaded)
    forward_block(1)
    send_blocks(2)

    @pl.loop(0, units + 1)
    def _(now):
        @pl.when((now > 0) & (now + 1 < units))
        def _():
            send_foreign(now + 1)

        @pl.when(now < units)
        def _():
            multiply(now)

        @pl.when(now >= 1)
        def _():
            finish(now - 1)

        @pl.when(now == 0)
        def _():
            spread_foreign(now + 1)

        @pl.when(now + 2 < units)
        def _():
            forward_block(now + 2)

        @pl.when(now + 1 < units)
        def _():
            forward_foreign(now + 1)

        @pl.when(now + 3 < units)
        def _():
            send_blocks(now + 3)

        shuffle_some(EARLY + 2 * now, EARLY + 2 * now + 2)

    for site in range(STEPS):
        for at in range(strips):
            trade_all(site, at).wait_send()

    @pl.loop(1, units)
    def _(unit):
        for d in range(1, bonds):
            hop(unit, d).wait_send()

    for part in range(2):
        for d in range(1, bonds):
            first_hop(part, d).wait_send()

    for unit in range(units - 2, units):
        cross_part(unit).wait_send()
        for at in range(strips):
            reply(unit, at).wait_send()
    for chunk in range(chunks):
        store(chunk).wait()
        for d in range(1, bonds):
            total_up(chunk, d).wait()
    totals_ref[...] = gathered[0] + gathered[1] + gathered[2] + gathered[3]


def sample_sites(env_start, stored_sites, slab_order, chosen):
    groups, bonds = slab_order.shape[1], lax.axis_size("bond")
    slab, outcomes, width = stored_sites.shape[2:]
    samples = env_start.shape[0]
    rows = samples // PARTS_OF_SITE
    units = STEPS * PARTS_OF_SITE
    wide, strip = min(width, 128), min(width, 256)
    strips = width // strip
    kind = env_start.dtype
    dma = pltpu.SemaphoreType.DMA
    selected, totals = pl.pallas_call(
        functools.partial(sampling_kernel, bonds, groups),
        in_specs=[
            pl.BlockSpec(memory_space=pltpu.SMEM),
            pl.BlockSpec(memory_space=pl.ANY),
            pl.BlockSpec(memory_space=pl.ANY),
            pl.BlockSpec(memory_space=pltpu.VMEM),
        ],
        out_specs=(pl.BlockSpec(memory_space=pl.ANY), pl.BlockSpec(memory_space=pltpu.VMEM)),
        out_shape=(
            jax.ShapeDtypeStruct((samples, width), jnp.float32),
            jax.ShapeDtypeStruct((STEPS * outcomes, samples), jnp.float32),
        ),
        scratch_shapes=[
            pltpu.VMEM((STEPS, 2, outcomes, slab, width), kind),
            pltpu.VMEM((STEPS, bonds, samples, width), kind),
            pltpu.VMEM((PARTS_OF_SITE, 2, rows, width), kind),
            pltpu.VMEM((2, 2, rows, width), kind),
            pltpu.VMEM((2, strips, outcomes, rows, strip), kind),
            pltpu.VMEM((PARTS_OF_SITE, strips, outcomes, rows, strip), kind),
            pltpu.VMEM((2, strips, outcomes, rows, strip), jnp.float32),
            pltpu.VMEM((2, 2 * rows, width), kind),
            pltpu.VMEM((2, slab, outcomes, wide), kind),
            pltpu.VMEM((samples, 128), jnp.float32),
            pltpu.VMEM((bonds, STEPS * outcomes, samples), jnp.float32),
            pltpu.VMEM((STEPS, samples, 128), jnp.int32),
            pltpu.VMEM((samples, width), jnp.float32),
            dma,
            dma((2,)),
            dma((STEPS, strips)),
            dma((STEPS, strips)),
            dma((units + 1, bonds - 1)),
            dma((units + 1, bonds - 1)),
            dma((units + 1,)),
            dma((units + 1,)),
            dma((units, bonds - 1)),
            dma((units, bonds - 1)),
            dma((units, strips)),
            dma((units, strips)),
            dma((PARTS_OF_SITE, bonds - 1)),
            dma((PARTS_OF_SITE, bonds - 1)),
            dma((PARTS_OF_SITE,)),
        ],
        compiler_params=pltpu.CompilerParams(
            collective_id=0, has_side_effects=True, vmem_limit_bytes=67_000_000
        ),
    )(slab_order, env_start, stored_sites, jnp.transpose(chosen))
    totals = jnp.transpose(totals).reshape(samples, STEPS, outcomes)
    factor = jnp.ones((samples,), jnp.float32)
    labels = jnp.arange(outcomes, dtype=jnp.int32)
    probabilities = []
    for site in range(STEPS):
        scaled = totals[:, site] * (factor * factor)[:, None]
        probabilities.append(scaled / jnp.sum(scaled, axis=1, keepdims=True))
        hit = chosen[:, site][:, None] == labels[None, :]
        factor = factor * lax.rsqrt(jnp.sum(jnp.where(hit, scaled, 0.0), axis=1) / (width * bonds) + epsilon)
    return jnp.stack(probabilities, axis=1), selected * factor[:, None]


def body(*arrays):
    return compute(*arrays)


def solution(mesh):
    fused = mesh.shape["samp"] == 4 and mesh.shape["bond"] == 4
    return jax.shard_map(
        sample_sites if fused else body,
        mesh=mesh,
        in_specs=(
            P(("parts", "samp"), "bond"),
            P("parts", "samp", None, None, "bond"),
            P("parts", None),
            P(("parts", "samp"), None),
        ),
        out_specs=(P(("parts", "samp"), None, None), P(("parts", "samp"), "bond")),
        check_vma=False,
    )
```
